512 devices in a mesh: gx: 8 (over y_hi, core), gy: 8 (over z), gz: 8 (over y_lo, x).
Axes of the slice: x: 4, y: 8 (y_hi: 4, y_lo: 2; y = y_hi * 2 + y_lo), z: 8, core: 2. Of those that a mesh axis runs over, the one named last changes fastest.
Arguments:
- velocity: float32 [256, 256, 1024], P('gx', 'gy', 'gz'), may hold values from -6 to 6
- marker_logvisc: float32 [65536, 128], P(('gx', 'gy', 'gz')), may hold values from -3 to 3
- marker_force: float32 [65536, 128], P(('gx', 'gy', 'gz')), may hold values from -6 to 6
- marker_weight: float32 [65536, 128], P(('gx', 'gy', 'gz')), may hold values from 0.5 to 2
- marker_cell: int32 [65536, 128], P(('gx', 'gy', 'gz')), may hold values from 0 to 127
- block_count: int32 [65536], P(('gx', 'gy', 'gz')), may hold values from 1 to 128, 6291456 in all
- block_owner: int32 [65536, 1], P(('gx', 'gy', 'gz')), may hold values from 0 to 63; in each aligned block of 128 rows (0 to 127, 128 to 255, ...) at most 4 rows name the same one
- block_tile: int32 [65536], P(('gx', 'gy', 'gz')), may hold values from 0 to 1023
- eig_low: float32 [1], replicated, may hold values from 0.05 to 0.3
- eig_high: float32 [1], replicated, may hold values from 1.5 to 2.2
Outputs:
- smoothed: float32 [256, 256, 1024], P('gx', 'gy', 'gz')
- marker_velocity: float32 [65536, 128], P(('gx', 'gy', 'gz'))
The draws below stay inside these ranges and needn't reach their ends.
Inputs may be any that keep to these rules, and one draw needn't show every extreme that they name: `block_owner`: among the 128 blocks of one device, no owner index is named by more than 4 blocks, a bound that some block reaches. `block_count`: slots at or after a block's count are padding; some block is full.
All inputs are finite; a program needn't handle non-finite values.
Results may differ from the reference program's by a relative error of at most 0.00017.
Values sent between devices are 32-bit elements; how exact they have to be, the bound alone decides.
A program may use at most 128 MiB of HBM per device.

```python
import math
import jax
import jax.numpy as jnp
import numpy as np

CX = 32
CY = 32
CZ = 128
NB = 128
BS = 128
TILE_X = 4
TILE_Y = 4
TILE_Z = 8
SWEEPS = 3
TILE_CELLS = 128
TILES_DEV = 1024
OWNERS = 64
CAP = 4
BLOCKS = 65536
NX = 256
NY = 256
NZ = 1024
N_GY = 8
N_GZ = 8


def place_ends(drawn, rng, least, high):
    index_at = [jax.random.randint(jax.random.fold_in(rng, axis), (), 0, length) for axis, length in enumerate(drawn.shape)]
    main_axis = drawn.shape.index(max(drawn.shape))
    beside = index_at[:main_axis] + [(index_at[main_axis] + 1) % drawn.shape[main_axis]] + index_at[main_axis + 1:]
    return drawn.at[tuple(index_at)].set(least).at[tuple(beside)].set(high)


def block_scale(key, shape, cuts, low, high):
    factor_of, own = 1.0, jax.random.fold_in(key, 6)
    for position, blocks in cuts:
        draws = jnp.exp(jax.random.uniform(jax.random.fold_in(own, position), (blocks,), jnp.float32, low / len(cuts), high / len(cuts)))
        factor_of = factor_of * jnp.repeat(draws, shape[position] // blocks).reshape([-1 if axis == position else 1 for axis in range(len(shape))])
    return factor_of


def split_up(count, total, reach, slope):
    loads = [(1 << 20) // math.isqrt(standing ** slope) + 1 for standing in range(2, count + 1)]
    spare, counts = total - reach - (count - 1), [1] * (count - 1)
    while spare > 0:
        free = [i for i in range(count - 1) if counts[i] < reach]
        pool, budget = sum([loads[i] for i in free]), spare
        for i in free:
            more = min(reach - counts[i], max(1, budget * loads[i] // pool), spare)
            counts[i] = counts[i] + more
            spare = spare - more
    return np.array([reach] + counts)


def ragged(rng, count, total, most, lean):
    if count == 2:
        one = jax.random.randint(rng, (), max(1, total - most), min(most, total - 1) + 1)
        return jnp.stack([one, total - one])
    sizes = jnp.asarray(split_up(count, total, most, lean), jnp.int32)
    twos = (count - 1) // 2
    source_of, sink = sizes[1:1 + 2 * twos:2], sizes[2:2 + 2 * twos:2]
    slack = jnp.minimum(source_of - 1, most - sink)
    moved = jax.random.randint(jax.random.fold_in(rng, 1), (twos,), 0, 1 << 20) % (slack + 1)
    sizes = sizes.at[1:1 + 2 * twos:2].set(source_of - moved).at[2:2 + 2 * twos:2].set(sink + moved)
    return sizes[jax.random.permutation(jax.random.fold_in(rng, 2), count)]


def shared_out(stream_key, own, number, rows, number_of, top, most, slope):
    order = jax.random.permutation(stream_key, number_of)
    heavy_load, usual = shares(number_of, rows * top, most, slope, True), shares(number_of, rows * top, most, slope, False)
    places = jnp.arange(number_of)

    def named(lengths, rotation):
        used = int((lengths > 0).sum())
        fixed = max(1, used // 4)
        moved = fixed + (places - fixed + rotation * (used - fixed)) % max(1, number_of - fixed)
        return jnp.zeros((number_of,), jnp.int32).at[order[jnp.where(places < fixed, places, moved)]].set(jnp.asarray(lengths, jnp.int32))

    lengths = jnp.where(number % 4 == 0, named(heavy_load, number // 4), named(usual, number - number // 4 - 1))
    mixed = jax.random.permutation(jax.random.fold_in(own, 3), number_of)
    source_of, receiver = mixed[0:number_of // 2 * 2:2], mixed[1:number_of // 2 * 2:2]
    slack = jnp.minimum(lengths[source_of] - 1, most - lengths[receiver]) // 2
    slack = jnp.where((source_of == order[0]) | (receiver == order[0]) | (lengths[receiver] == 0), 0, jnp.maximum(slack, 0))
    moved = jax.random.randint(jax.random.fold_in(own, 4), (number_of // 2,), 0, 1 << 20) % (slack + 1)
    lengths = lengths.at[source_of].add(-moved).at[receiver].add(moved)
    members = jnp.searchsorted(jnp.cumsum(lengths), jnp.arange(rows * top), side="right").astype(jnp.int32)
    grid = members.reshape(top, rows).T
    grid = grid[jax.random.permutation(jax.random.fold_in(own, 1), rows)]
    rotation = jax.random.randint(jax.random.fold_in(own, 2), (rows, 1), 0, top)
    return jnp.take_along_axis(grid, (jnp.arange(top)[None, :] + rotation) % top, axis=1)


def shares(amount, total, most, slope, full):
    weights = [(1 << 20) // math.isqrt(standing ** slope) + 1 for standing in range(1, amount + 1)]
    largest = most if full else min(most, max(-(-total // amount), total * weights[0] // sum(weights)))
    least = 1 if total - largest >= amount - 1 else 0
    counts, spare = [largest] + [least] * (amount - 1), total - largest - least * (amount - 1)
    while spare > 0:
        free = [i for i in range(1, amount) if counts[i] < largest] or [i for i in range(1, amount) if counts[i] < most]
        pool, left = sum([weights[i] for i in free]), spare
        for i in free:
            more = min(most - counts[i], max(1, left * weights[i] // pool), spare)
            counts[i] = counts[i] + more
            spare = spare - more
    return np.array(counts)


def centred(own_key, shape, spread, reach, pieces=(), held_as=jnp.bfloat16):
    gain = block_scale(own_key, shape, pieces, -0.22, 0.18) if pieces else 1.0
    drawn = jax.random.normal(own_key, shape, jnp.float32) * spread * gain
    return jnp.minimum(jnp.maximum(drawn, -reach), reach).astype(held_as)


def setup_inputs(seed: int = 0) -> dict:
    splits = jax.random.split(jax.random.key(seed), 11)
    velocity = centred(splits[0], (NX, NY, NZ), 1.0, 6.0, ((0, 8), (1, 8), (2, 8)), jnp.float32)
    marker_logvisc = jnp.clip(jax.random.uniform(splits[1], (BLOCKS, BS), jnp.float32, -3.0, 3.0) * block_scale(splits[1], (BLOCKS, BS), ((0, 512),), -0.4, 0.0), -3.0, 3.0)
    marker_force = centred(splits[2], (BLOCKS, BS), 1.0, 6.0, ((0, 512),), jnp.float32)
    marker_weight = jnp.clip(jnp.exp(math.log(2.0) - 1.3862944 * jax.random.uniform(splits[3], (BLOCKS, BS), jnp.float32) ** block_scale(splits[3], (BLOCKS, BS), ((0, 512),), -0.2, 0.2)), 0.5, 2.0)
    marker_cell = place_ends(jax.random.randint(splits[4], (BLOCKS, BS), 0, TILE_CELLS), jax.random.fold_in(splits[4], 1), 0, TILE_CELLS - 1).astype(jnp.int32)
    block_count = ragged(splits[5], BLOCKS, BLOCKS * BS * 3 // 4, BS, 0).astype(jnp.int32)
    block_owner_keys = jax.random.split(jax.random.fold_in(splits[6], 1), BLOCKS // NB)
    block_owner_turns = jax.random.permutation(jax.random.fold_in(splits[6], 3), BLOCKS // NB)
    block_owner = jax.vmap(lambda own, number: shared_out(jax.random.fold_in(splits[6], 2), own, number, NB, OWNERS, 1, CAP, 1))(block_owner_keys, block_owner_turns).reshape((BLOCKS, 1))
    block_tile = place_ends(jax.random.randint(splits[7], (BLOCKS,), 0, TILES_DEV), jax.random.fold_in(splits[7], 1), 0, TILES_DEV - 1).astype(jnp.int32)
    eig_low = jnp.clip(jax.random.uniform(splits[8], (1,), jnp.float32, 0.05, 0.3), 0.05, 0.3)
    eig_high = jnp.clip(jax.random.uniform(splits[9], (1,), jnp.float32, 1.5, 2.2), 1.5, 2.2)
    return dict(velocity=velocity, marker_logvisc=marker_logvisc, marker_force=marker_force, marker_weight=marker_weight, marker_cell=marker_cell, block_count=block_count, block_owner=block_owner, block_tile=block_tile, eig_low=eig_low, eig_high=eig_high)


def shifted(array, along, offset):
    index = [slice(1, extent - 1) for extent in array.shape]
    index[along] = slice(1 + offset, array.shape[along] - 1 + offset)
    return array[tuple(index)]


def operate(field, viscosity):
    centre_visc = shifted(viscosity, 0, 0)
    centre_field = shifted(field, 0, 0)
    flux_total = jnp.zeros_like(centre_field)
    diagonal = jnp.zeros_like(centre_field)
    for along in range(3):
        for offset in (1, -1):
            face = 0.5 * (centre_visc + shifted(viscosity, along, offset))
            diagonal = diagonal + face
            flux_total = flux_total + face * (centre_field - shifted(field, along, offset))
    return flux_total, diagonal


def reference(velocity, marker_logvisc, marker_force, marker_weight, marker_cell, block_count, block_owner, block_tile, eig_low, eig_high):
    owners = N_GY * N_GZ
    blocks = jnp.arange(BLOCKS, dtype=jnp.int32)
    column = blocks // NB // owners
    owner = block_owner[:, 0]
    own_y = owner // N_GZ
    own_z = owner % N_GZ
    tiles_y = CY // TILE_Y
    tiles_z = CZ // TILE_Z
    tile_x = block_tile // (tiles_y * tiles_z)
    tile_y = (block_tile // tiles_z) % tiles_y
    tile_z = block_tile % tiles_z
    cell_x = marker_cell // (TILE_Y * TILE_Z)
    cell_y = (marker_cell // TILE_Z) % TILE_Y
    cell_z = marker_cell % TILE_Z
    coord_x = (column * CX + tile_x * TILE_X)[:, None] + cell_x
    coord_y = (own_y * CY + tile_y * TILE_Y)[:, None] + cell_y
    coord_z = (own_z * CZ + tile_z * TILE_Z)[:, None] + cell_z
    flat = ((coord_x * NY + coord_y) * NZ + coord_z).astype(jnp.int32).ravel()
    live = jnp.arange(BS, dtype=jnp.int32)[None, :] < block_count[:, None]
    weight = jnp.where(live, marker_weight, jnp.zeros_like(marker_weight))
    cells = NX * NY * NZ
    weight_sum = jax.ops.segment_sum(weight.ravel(), flat, cells).reshape(NX, NY, NZ)
    log_sum = jax.ops.segment_sum((weight * marker_logvisc).ravel(), flat, cells).reshape(NX, NY, NZ)
    rhs = jax.ops.segment_sum((weight * marker_force).ravel(), flat, cells).reshape(NX, NY, NZ)
    viscosity = jnp.exp(log_sum / (1.0 + weight_sum))
    visc_pad = jnp.pad(viscosity, 1)
    low = eig_low[0]
    high = eig_high[0]
    centre = (high + low) / 2
    half_width = (high - low) / 2
    sigma_ratio = centre / half_width
    rho_now = 1.0 / sigma_ratio
    field = velocity
    update = jnp.zeros_like(velocity)
    for sweep_index in range(SWEEPS):
        flux_total, diagonal = operate(jnp.pad(field, 1), visc_pad)
        resid = rhs - flux_total
        if sweep_index == 0:
            update = resid / diagonal / centre
        else:
            rho_next = 1.0 / (2.0 * sigma_ratio - rho_now)
            update = rho_next * rho_now * update + (2.0 * rho_next / half_width) * (resid / diagonal)
            rho_now = rho_next
        field = field + update
    picked = field.ravel()[flat].reshape(BLOCKS, BS)
    marker_velocity = jnp.where(live, picked, jnp.zeros_like(picked))
    return field, marker_velocity
```

```python
import functools
import math

import jax
import jax.numpy as jnp
from jax import lax
from jax.experimental import pallas as pl
from jax.experimental.pallas import tpu as pltpu
from jax.sharding import PartitionSpec as P

TILE_CELLS = 128
SWEEPS = 3
EX, EY, EZ = 32, 32, 128
TILES = 1024
SIDES = (("gx", 1), ("gx", -1), ("gy", 1), ("gy", -1), ("gz", 1), ("gz", -1))
FACE_SHAPES = ((EY, EZ), (EY, EZ), (EX, EZ), (EX, EZ), (EY, EX), (EY, EX))
VMEM = pltpu.MemorySpace.VMEM
SMEM = pltpu.MemorySpace.SMEM


def swap_blocks(t):
    row = lax.broadcasted_iota(jnp.int32, t.shape, 0)
    lane = lax.broadcasted_iota(jnp.int32, t.shape, 1)
    for k in range(4):
        s = 1 << k
        row_bit = (row >> k) & 1
        lane_bit = (lane >> (3 + k)) & 1
        a = pltpu.roll(pltpu.roll(t, 128 - s, 0), 8 * s, 1)
        b = pltpu.roll(pltpu.roll(t, s, 0), 128 - 8 * s, 1)
        t = jnp.where(row_bit == lane_bit, t, jnp.where(row_bit == 0, a, b))
    return t


def pack_kernel(flat_ref, tile_ref, sums_ref, out_ref):
    owners = out_ref.shape[0]
    rows = owners * 8
    row = lax.broadcasted_iota(jnp.int32, (rows, 128), 0)
    key = (row >> 3) * 4 + (row & 3)
    pick = (key == flat_ref[...]).astype(jnp.float32)
    low = (row & 7) < 4

    def take(values):
        return jnp.dot(
            pick, values, precision=lax.Precision.HIGHEST, preferred_element_type=jnp.float32
        )

    top = jnp.where(low, take(sums_ref[0]), take(sums_ref[1]))
    bottom = jnp.where(low, take(sums_ref[2]), take(tile_ref[...]))
    out_ref[:, 0:8, :] = top.reshape(owners, 8, 128)
    out_ref[:, 8:16, :] = bottom.reshape(owners, 8, 128)


def put_faces(read, faces, index):
    lane = lax.broadcasted_iota(jnp.int32, (EY, EX), 1)
    low = jnp.zeros((EY, EX), jnp.float32)
    high = jnp.zeros((EY, EX), jnp.float32)
    for x in range(EX):
        plane = read(x)
        low = jnp.where(lane == x, plane[:, 0:1], low)
        high = jnp.where(lane == x, plane[:, EZ - 1 : EZ], high)
        if x == 0:
            faces[1][index] = plane
        if x == EX - 1:
            faces[0][index] = plane
        faces[3][index, x : x + 1, :] = plane[0:1]
        faces[2][index, x : x + 1, :] = plane[EY - 1 : EY]
    faces[5][index] = low
    faces[4][index] = high


def grid_kernel(tile_ref, inc_ref, vel_ref, visc_ref, rhs_ref, *rest):
    faces, (acc_ref,) = rest[:6], rest[6:]
    acc_ref[...] = jnp.zeros_like(acc_ref)

    def add(owner, carry):
        for slot in range(4):
            tile = tile_ref[owner * 4 + slot]
            for c in range(3):
                acc_ref[c, pl.ds(tile, 1), :] += inc_ref[owner, 4 * c + slot : 4 * c + slot + 1, :]
        return carry

    lax.fori_loop(0, inc_ref.shape[0], add, 0)

    def spread(tx, carry):
        rows = pl.ds(pl.multiple_of(tx * 128, 128), 128)
        visc = jnp.exp(acc_ref[1, rows, :] / (1.0 + acc_ref[0, rows, :]))
        for values, out in ((visc, visc_ref), (acc_ref[2, rows, :], rhs_ref)):
            values = swap_blocks(values)
            for ty in range(8):
                for cx in range(4):
                    start = ty * 16 + cx * 4
                    out[tx * 4 + cx, ty * 4 : ty * 4 + 4, :] = values[start : start + 4]
        return carry

    lax.fori_loop(0, 8, spread, 0)
    put_faces(lambda x: visc_ref[x], faces, 0)
    put_faces(lambda x: vel_ref[x], faces, 1)


def sweep_kernel(first, last, coef_ref, field_ref, rhs_ref, visc_ref, *rest):
    visc_faces, rest = rest[:6], rest[6:]
    if first:
        field_faces, field_index = visc_faces, 1
    else:
        field_faces, rest = rest[:6], rest[6:]
        field_index = 0
        old_ref, rest = rest[0], rest[1:]
    out_ref, rest = rest[0], rest[1:]
    row = lax.broadcasted_iota(jnp.int32, (EY, EZ), 0)
    lane = lax.broadcasted_iota(jnp.int32, (EY, EZ), 1)

    def around(ref, faces, index, x):
        plane = ref[x]
        return (
            ref[x - 1] if x > 0 else faces[0][index],
            ref[x + 1] if x < EX - 1 else faces[1][index],
            jnp.where(row == 0, faces[2][index, x : x + 1, :], pltpu.roll(plane, 1, 0)),
            jnp.where(row == EY - 1, faces[3][index, x : x + 1, :], pltpu.roll(plane, EY - 1, 0)),
            jnp.where(lane == 0, faces[4][index, :, x : x + 1], pltpu.roll(plane, 1, 1)),
            jnp.where(lane == EZ - 1, faces[5][index, :, x : x + 1], pltpu.roll(plane, EZ - 1, 1)),
        )

    for x in range(EX):
        field = field_ref[x]
        visc = visc_ref[x]
        flux = jnp.zeros_like(field)
        diagonal = jnp.zeros_like(field)
        for near_visc, near_field in zip(
            around(visc_ref, visc_faces, 0, x), around(field_ref, field_faces, field_index, x)
        ):
            face = 0.5 * (visc + near_visc)
            diagonal = diagonal + face
            flux = flux + face * (field - near_field)
        update = coef_ref[1] * ((rhs_ref[x] - flux) / diagonal)
        if not first:
            update = coef_ref[0] * old_ref[x] + update
        out_ref[x] = field + update
        if not last:
            rest[0][x] = update
    if not last:
        put_faces(lambda x: out_ref[x], rest[1:7], 0)
        return
    tiles_ref, buffer = rest

    def gather(tx, carry):
        for ty in range(8):
            for cx in range(4):
                start = ty * 16 + cx * 4
                buffer[start : start + 4, :] = out_ref[tx * 4 + cx, ty * 4 : ty * 4 + 4, :]
        tiles_ref[pl.ds(pl.multiple_of(tx * 128, 128), 128), :] = swap_blocks(buffer[...])
        return carry

    lax.fori_loop(0, 8, gather, 0)


def call(kernel, outs, specs, args, scratch=()):
    return pl.pallas_call(
        kernel,
        out_shape=[jax.ShapeDtypeStruct(s, jnp.float32) for s in outs],
        in_specs=[pl.BlockSpec(memory_space=s) for s in specs],
        out_specs=[pl.BlockSpec(memory_space=VMEM)] * len(outs),
        scratch_shapes=[pltpu.VMEM(s, jnp.float32) for s in scratch],
        compiler_params=pltpu.CompilerParams(vmem_limit_bytes=40 * 1024 * 1024),
    )(*args)


def exchange(faces):
    received = []
    for face, (axis, step) in zip(faces, SIDES):
        ends = lax.axis_size(axis) - 1
        if step == 1:
            pairs = [(i, i + 1) for i in range(ends)]
        else:
            pairs = [(i + 1, i) for i in range(ends)]
        received.append(lax.ppermute(face, axis, pairs))
    return received


def smooth(velocity, rhs, viscosity, faces, low, high):
    centre = (high + low) / 2
    half_width = (high - low) / 2
    sigma_ratio = centre / half_width
    rho_now = 1.0 / sigma_ratio
    grid = (EX, EY, EZ)
    visc_faces = exchange(faces)
    field, update, field_faces = velocity, None, None
    for index in range(SWEEPS):
        first, last = index == 0, index == SWEEPS - 1
        args = [field, rhs, viscosity, *visc_faces]
        if first:
            coef = jnp.stack([jnp.zeros_like(centre), 1.0 / centre])
        else:
            rho_next = 1.0 / (2.0 * sigma_ratio - rho_now)
            coef = jnp.stack([rho_next * rho_now, 2.0 * rho_next / half_width])
            rho_now = rho_next
            args += [*field_faces, update]
        outs = [grid, (TILES, 128)] if last else [grid, grid] + [(1, *s) for s in FACE_SHAPES]
        results = call(
            functools.partial(sweep_kernel, first, last),
            outs,
            [SMEM] + [VMEM] * len(args),
            [coef, *args],
            [(128, 128)] if last else [],
        )
        if last:
            return results
        field, update = results[:2]
        field_faces = exchange(results[2:])


def one_hot_cells(cells):
    return (cells[..., None] == jnp.arange(TILE_CELLS, dtype=jnp.int32)).astype(jnp.float32)


def body(
    velocity,
    marker_logvisc,
    marker_force,
    marker_weight,
    marker_cell,
    block_count,
    block_owner,
    block_tile,
    eig_low,
    eig_high,
):
    blocks, slots = marker_weight.shape
    owners = lax.axis_size("gy") * lax.axis_size("gz")
    capacity = 4
    group = math.gcd(blocks, 64)
    groups = blocks // group
    live = jnp.arange(slots, dtype=jnp.int32)[None, :] < block_count[:, None]
    weight = jnp.where(live, marker_weight, 0.0)
    channels = jnp.stack([weight, weight * marker_logvisc, weight * marker_force])
    channels = channels.reshape(3, groups, group, slots).transpose(1, 0, 2, 3)
    cells_grouped = marker_cell.reshape(groups, group, slots)

    def project(pair):
        cells, values = pair
        return jnp.einsum(
            "gsk,cgs->gck", one_hot_cells(cells), values, precision=lax.Precision.HIGHEST
        )

    block_sums = lax.map(project, (cells_grouped, channels)).reshape(blocks, 3, TILE_CELLS)
    block_sums = block_sums.transpose(1, 0, 2)
    owner = block_owner[:, 0]
    member = (owner[:, None] == jnp.arange(owners, dtype=jnp.int32)[None, :]).astype(jnp.int32)
    slot_of = jnp.sum(jnp.cumsum(member, axis=0) * member, axis=1) - 1
    flat = owner * capacity + slot_of
    tile_wide = jnp.broadcast_to(block_tile.astype(jnp.float32)[:, None], (blocks, 128))
    (outgoing,) = call(
        pack_kernel, [(owners, 16, 128)], [VMEM] * 3, [flat[None, :], tile_wide, block_sums]
    )
    incoming = lax.all_to_all(outgoing, ("gy", "gz"), split_axis=0, concat_axis=0, tiled=True)
    tile_in = incoming[:, 12:16, 0].astype(jnp.int32).reshape(owners * capacity)
    results = call(
        grid_kernel,
        [(EX, EY, EZ)] * 2 + [(2, *s) for s in FACE_SHAPES],
        [SMEM, VMEM, VMEM],
        [tile_in, incoming, velocity],
        [(3, TILES, 128)],
    )
    viscosity, rhs = results[:2]
    smoothed, tile_view = smooth(velocity, rhs, viscosity, results[2:], eig_low[0], eig_high[0])
    returning = tile_view[tile_in].reshape(owners, capacity, TILE_CELLS)
    arrived = lax.all_to_all(returning, ("gy", "gz"), split_axis=0, concat_axis=0, tiled=True)
    block_values = arrived[owner, slot_of].reshape(groups, group, TILE_CELLS)

    def interpolate(pair):
        cells, values = pair
        return jnp.einsum(
            "gsk,gk->gs", one_hot_cells(cells), values, precision=lax.Precision.HIGHEST
        )

    picked = lax.map(interpolate, (cells_grouped, block_values)).reshape(blocks, slots)
    marker_velocity = jnp.where(live, picked, 0.0)
    return (smoothed, marker_velocity)


def solution(mesh):
    return jax.shard_map(
        body,
        mesh=mesh,
        in_specs=(
            P("gx", "gy", "gz"),
            P(("gx", "gy", "gz"), None),
            P(("gx", "gy", "gz"), None),
            P(("gx", "gy", "gz"), None),
            P(("gx", "gy", "gz"), None),
            P(("gx", "gy", "gz")),
            P(("gx", "gy", "gz"), None),
            P(("gx", "gy", "gz")),
            P(),
            P(),
        ),
        out_specs=(P("gx", "gy", "gz"), P(("gx", "gy", "gz"), None)),
        check_vma=False,
    )
```

```python
import functools
import math

import jax
import jax.numpy as jnp
from jax import lax
from jax.experimental import pallas as pl
from jax.experimental.pallas import tpu as pltpu
from jax.sharding import PartitionSpec as P

TILE_CELLS = 128
SWEEPS = 3
EX, EY, EZ = 32, 32, 128
TILES = 1024
SIDES = (("gx", 1), ("gx", -1), ("gy", 1), ("gy", -1), ("gz", 1), ("gz", -1))
FACE_SHAPES = ((EY, EZ), (EY, EZ), (EX, EZ), (EX, EZ), (EY, EX), (EY, EX))
VMEM = pltpu.MemorySpace.VMEM
SMEM = pltpu.MemorySpace.SMEM


def swap_blocks(t):
    row = lax.broadcasted_iota(jnp.int32, t.shape, 0)
    lane = lax.broadcasted_iota(jnp.int32, t.shape, 1)
    for k in range(4):
        s = 1 << k
        row_bit = (row >> k) & 1
        lane_bit = (lane >> (3 + k)) & 1
        a = pltpu.roll(pltpu.roll(t, 128 - s, 0), 8 * s, 1)
        b = pltpu.roll(pltpu.roll(t, s, 0), 128 - 8 * s, 1)
        t = jnp.where(row_bit == lane_bit, t, jnp.where(row_bit == 0, a, b))
    return t


def pack_kernel(flat_ref, tile_ref, sums_ref, out_ref):
    owners = out_ref.shape[0]
    rows = owners * 8
    row = lax.broadcasted_iota(jnp.int32, (rows, 128), 0)
    key = (row >> 3) * 4 + (row & 3)
    pick = (key == flat_ref[...]).astype(jnp.float32)
    low = (row & 7) < 4

    def take(values):
        return jnp.dot(
            pick, values, precision=lax.Precision.HIGHEST, preferred_element_type=jnp.float32
        )

    top = jnp.where(low, take(sums_ref[0]), take(sums_ref[1]))
    bottom = jnp.where(low, take(sums_ref[2]), take(tile_ref[...]))
    out_ref[:, 0:8, :] = top.reshape(owners, 8, 128)
    out_ref[:, 8:16, :] = bottom.reshape(owners, 8, 128)


def put_faces(read, faces, index):
    lane = lax.broadcasted_iota(jnp.int32, (EY, EX), 1)
    low = jnp.zeros((EY, EX), jnp.float32)
    high = jnp.zeros((EY, EX), jnp.float32)
    for x in range(EX):
        plane = read(x)
        low = jnp.where(lane == x, plane[:, 0:1], low)
        high = jnp.where(lane == x, plane[:, EZ - 1 : EZ], high)
        if x == 0:
            faces[1][index] = plane
        if x == EX - 1:
            faces[0][index] = plane
        faces[3][index, x : x + 1, :] = plane[0:1]
        faces[2][index, x : x + 1, :] = plane[EY - 1 : EY]
    faces[5][index] = low
    faces[4][index] = high


def grid_kernel(tile_ref, inc_ref, vel_ref, visc_ref, rhs_ref, *rest):
    faces, (acc_ref,) = rest[:6], rest[6:]
    acc_ref[...] = jnp.zeros_like(acc_ref)

    def add(owner, carry):
        for slot in range(4):
            tile = tile_ref[owner * 4 + slot]
            for c in range(3):
                acc_ref[c, pl.ds(tile, 1), :] += inc_ref[owner, 4 * c + slot : 4 * c + slot + 1, :]
        return carry

    lax.fori_loop(0, inc_ref.shape[0], add, 0)

    def spread(tx, carry):
        rows = pl.ds(pl.multiple_of(tx * 128, 128), 128)
        visc = jnp.exp(acc_ref[1, rows, :] / (1.0 + acc_ref[0, rows, :]))
        for values, out in ((visc, visc_ref), (acc_ref[2, rows, :], rhs_ref)):
            values = swap_blocks(values)
            for ty in range(8):
                for cx in range(4):
                    start = ty * 16 + cx * 4
                    out[tx * 4 + cx, ty * 4 : ty * 4 + 4, :] = values[start : start + 4]
        return carry

    lax.fori_loop(0, 8, spread, 0)
    put_faces(lambda x: visc_ref[x], faces, 0)
    put_faces(lambda x: vel_ref[x], faces, 1)


def sweep_kernel(first, last, coef_ref, field_ref, rhs_ref, visc_ref, *rest):
    visc_faces, rest = rest[:6], rest[6:]
    if first:
        field_faces, field_index = visc_faces, 1
    else:
        field_faces, rest = rest[:6], rest[6:]
        field_index = 0
        old_ref, rest = rest[0], rest[1:]
    out_ref, rest = rest[0], rest[1:]
    row = lax.broadcasted_iota(jnp.int32, (EY, EZ), 0)
    lane = lax.broadcasted_iota(jnp.int32, (EY, EZ), 1)

    def around(ref, faces, index, x):
        plane = ref[x]
        return (
            ref[x - 1] if x > 0 else faces[0][index],
            ref[x + 1] if x < EX - 1 else faces[1][index],
            jnp.where(row == 0, faces[2][index, x : x + 1, :], pltpu.roll(plane, 1, 0)),
            jnp.where(row == EY - 1, faces[3][index, x : x + 1, :], pltpu.roll(plane, EY - 1, 0)),
            jnp.where(lane == 0, faces[4][index, :, x : x + 1], pltpu.roll(plane, 1, 1)),
            jnp.where(lane == EZ - 1, faces[5][index, :, x : x + 1], pltpu.roll(plane, EZ - 1, 1)),
        )

    for x in range(EX):
        field = field_ref[x]
        visc = visc_ref[x]
        flux = jnp.zeros_like(field)
        diagonal = jnp.zeros_like(field)
        for near_visc, near_field in zip(
            around(visc_ref, visc_faces, 0, x), around(field_ref, field_faces, field_index, x)
        ):
            face = 0.5 * (visc + near_visc)
            diagonal = diagonal + face
            flux = flux + face * (field - near_field)
        update = coef_ref[1] * ((rhs_ref[x] - flux) / diagonal)
        if not first:
            update = coef_ref[0] * old_ref[x] + update
        out_ref[x] = field + update
        if not last:
            rest[0][x] = update
    if not last:
        put_faces(lambda x: out_ref[x], rest[1:7], 0)
        return
    tiles_ref, buffer = rest

    def gather(tx, carry):
        for ty in range(8):
            for cx in range(4):
                start = ty * 16 + cx * 4
                buffer[start : start + 4, :] = out_ref[tx * 4 + cx, ty * 4 : ty * 4 + 4, :]
        tiles_ref[pl.ds(pl.multiple_of(tx * 128, 128), 128), :] = swap_blocks(buffer[...])
        return carry

    lax.fori_loop(0, 8, gather, 0)


def call(kernel, outs, specs, args, scratch=()):
    return pl.pallas_call(
        kernel,
        out_shape=[jax.ShapeDtypeStruct(s, jnp.float32) for s in outs],
        in_specs=[pl.BlockSpec(memory_space=s) for s in specs],
        out_specs=[pl.BlockSpec(memory_space=VMEM)] * len(outs),
        scratch_shapes=[pltpu.VMEM(s, jnp.float32) for s in scratch],
        compiler_params=pltpu.CompilerParams(vmem_limit_bytes=40 * 1024 * 1024),
    )(*args)


def halo_kernel(*refs):
    sources, landings, (send_sem, recv_sem) = refs[:6], refs[6:12], refs[12:]
    barrier = pltpu.get_barrier_semaphore()
    routes = []
    greeted = 0
    for axis, step in SIDES:
        count = lax.axis_size(axis)
        place = lax.axis_index(axis)
        above, below = place < count - 1, place > 0
        sends, receives = (above, below) if step == 1 else (below, above)
        routes.append((sends, receives, {axis: lax.rem(place + step + count, count)}))
        greeted = greeted + jnp.where(sends, 1, 0)
    for sends, _, target in routes:

        @pl.when(sends)
        def _greet():
            pl.semaphore_signal(
                barrier, inc=1, device_id=target, device_id_type=pl.DeviceIdType.MESH
            )

    pl.semaphore_wait(barrier, greeted)

    def copy(k):
        return pltpu.make_async_remote_copy(
            src_ref=sources[k],
            dst_ref=landings[k],
            send_sem=send_sem.at[k],
            recv_sem=recv_sem.at[k],
            device_id=routes[k][2],
            device_id_type=pl.DeviceIdType.MESH,
        )

    for k, (sends, receives, _) in enumerate(routes):

        @pl.when(sends)
        def _start():
            copy(k).start()

        @pl.when(jnp.logical_not(receives))
        def _outside():
            landings[k][...] = jnp.zeros_like(landings[k])

    for k, (sends, receives, _) in enumerate(routes):

        @pl.when(receives)
        def _landed():
            copy(k).wait_recv()

        @pl.when(sends)
        def _left():
            copy(k).wait_send()


def exchange(faces, index):
    return pl.pallas_call(
        halo_kernel,
        out_shape=[jax.ShapeDtypeStruct(f.shape, f.dtype) for f in faces],
        in_specs=[pl.BlockSpec(memory_space=VMEM)] * 6,
        out_specs=[pl.BlockSpec(memory_space=VMEM)] * 6,
        scratch_shapes=[pltpu.SemaphoreType.DMA((6,)), pltpu.SemaphoreType.DMA((6,))],
        compiler_params=pltpu.CompilerParams(collective_id=index, has_side_effects=True),
    )(*faces)


def smooth(velocity, rhs, viscosity, faces, low, high):
    centre = (high + low) / 2
    half_width = (high - low) / 2
    sigma_ratio = centre / half_width
    rho_now = 1.0 / sigma_ratio
    grid = (EX, EY, EZ)
    visc_faces = exchange(faces, 0)
    field, update, field_faces = velocity, None, None
    for index in range(SWEEPS):
        first, last = index == 0, index == SWEEPS - 1
        args = [field, rhs, viscosity, *visc_faces]
        if first:
            coef = jnp.stack([jnp.zeros_like(centre), 1.0 / centre])
        else:
            rho_next = 1.0 / (2.0 * sigma_ratio - rho_now)
            coef = jnp.stack([rho_next * rho_now, 2.0 * rho_next / half_width])
            rho_now = rho_next
            args += [*field_faces, update]
        outs = [grid, (TILES, 128)] if last else [grid, grid] + [(1, *s) for s in FACE_SHAPES]
        results = call(
            functools.partial(sweep_kernel, first, last),
            outs,
            [SMEM] + [VMEM] * len(args),
            [coef, *args],
            [(128, 128)] if last else [],
        )
        if last:
            return results
        field, update = results[:2]
        field_faces = exchange(results[2:], index + 1)


def one_hot_cells(cells):
    return (cells[..., None] == jnp.arange(TILE_CELLS, dtype=jnp.int32)).astype(jnp.float32)


def body(
    velocity,
    marker_logvisc,
    marker_force,
    marker_weight,
    marker_cell,
    block_count,
    block_owner,
    block_tile,
    eig_low,
    eig_high,
):
    blocks, slots = marker_weight.shape
    owners = lax.axis_size("gy") * lax.axis_size("gz")
    capacity = 4
    group = math.gcd(blocks, 64)
    groups = blocks // group
    live = jnp.arange(slots, dtype=jnp.int32)[None, :] < block_count[:, None]
    weight = jnp.where(live, marker_weight, 0.0)
    channels = jnp.stack([weight, weight * marker_logvisc, weight * marker_force])
    channels = channels.reshape(3, groups, group, slots).transpose(1, 0, 2, 3)
    cells_grouped = marker_cell.reshape(groups, group, slots)

    def project(pair):
        cells, values = pair
        return jnp.einsum(
            "gsk,cgs->gck", one_hot_cells(cells), values, precision=lax.Precision.HIGHEST
        )

    block_sums = lax.map(project, (cells_grouped, channels)).reshape(blocks, 3, TILE_CELLS)
    block_sums = block_sums.transpose(1, 0, 2)
    owner = block_owner[:, 0]
    member = (owner[:, None] == jnp.arange(owners, dtype=jnp.int32)[None, :]).astype(jnp.int32)
    slot_of = jnp.sum(jnp.cumsum(member, axis=0) * member, axis=1) - 1
    flat = owner * capacity + slot_of
    tile_wide = jnp.broadcast_to(block_tile.astype(jnp.float32)[:, None], (blocks, 128))
    (outgoing,) = call(
        pack_kernel, [(owners, 16, 128)], [VMEM] * 3, [flat[None, :], tile_wide, block_sums]
    )
    incoming = lax.all_to_all(outgoing, ("gy", "gz"), split_axis=0, concat_axis=0, tiled=True)
    tile_in = incoming[:, 12:16, 0].astype(jnp.int32).reshape(owners * capacity)
    results = call(
        grid_kernel,
        [(EX, EY, EZ)] * 2 + [(2, *s) for s in FACE_SHAPES],
        [SMEM, VMEM, VMEM],
        [tile_in, incoming, velocity],
        [(3, TILES, 128)],
    )
    viscosity, rhs = results[:2]
    smoothed, tile_view = smooth(velocity, rhs, viscosity, results[2:], eig_low[0], eig_high[0])
    returning = tile_view[tile_in].reshape(owners, capacity, TILE_CELLS)
    arrived = lax.all_to_all(returning, ("gy", "gz"), split_axis=0, concat_axis=0, tiled=True)
    block_values = arrived[owner, slot_of].reshape(groups, group, TILE_CELLS)

    def interpolate(pair):
        cells, values = pair
        return jnp.einsum(
            "gsk,gk->gs", one_hot_cells(cells), values, precision=lax.Precision.HIGHEST
        )

    picked = lax.map(interpolate, (cells_grouped, block_values)).reshape(blocks, slots)
    marker_velocity = jnp.where(live, picked, 0.0)
    return (smoothed, marker_velocity)


def solution(mesh):
    return jax.shard_map(
        body,
        mesh=mesh,
        in_specs=(
            P("gx", "gy", "gz"),
            P(("gx", "gy", "gz"), None),
            P(("gx", "gy", "gz"), None),
            P(("gx", "gy", "gz"), None),
            P(("gx", "gy", "gz"), None),
            P(("gx", "gy", "gz")),
            P(("gx", "gy", "gz"), None),
            P(("gx", "gy", "gz")),
            P(),
            P(),
        ),
        out_specs=(P("gx", "gy", "gz"), P(("gx", "gy", "gz"), None)),
        check_vma=False,
    )
```

```python
import functools
import math

import jax
import jax.numpy as jnp
from jax import lax
from jax.experimental import pallas as pl
from jax.experimental.pallas import tpu as pltpu
from jax.sharding import PartitionSpec as P

TILE_CELLS = 128
SWEEPS = 3
EX, EY, EZ = 32, 32, 128
TILES = 1024
SIDES = (("gx", 1), ("gx", -1), ("gy", 1), ("gy", -1), ("gz", 1), ("gz", -1))
FACE_SHAPES = ((EY, EZ), (EY, EZ), (EX, EZ), (EX, EZ), (EY, EX), (EY, EX))
VMEM = pltpu.MemorySpace.VMEM
SMEM = pltpu.MemorySpace.SMEM


def swap_blocks(t):
    row = lax.broadcasted_iota(jnp.int32, t.shape, 0)
    lane = lax.broadcasted_iota(jnp.int32, t.shape, 1)
    for k in range(4):
        s = 1 << k
        row_bit = (row >> k) & 1
        lane_bit = (lane >> (3 + k)) & 1
        a = pltpu.roll(pltpu.roll(t, 128 - s, 0), 8 * s, 1)
        b = pltpu.roll(pltpu.roll(t, s, 0), 128 - 8 * s, 1)
        t = jnp.where(row_bit == lane_bit, t, jnp.where(row_bit == 0, a, b))
    return t


def pack_kernel(flat_ref, tile_ref, sums_ref, out_ref):
    owners = out_ref.shape[0]
    rows = owners * 8
    row = lax.broadcasted_iota(jnp.int32, (rows, 128), 0)
    key = (row >> 3) * 4 + (row & 3)
    pick = (key == flat_ref[...]).astype(jnp.float32)
    low = (row & 7) < 4

    def take(values):
        return jnp.dot(
            pick, values, precision=lax.Precision.HIGHEST, preferred_element_type=jnp.float32
        )

    top = jnp.where(low, take(sums_ref[0]), take(sums_ref[1]))
    bottom = jnp.where(low, take(sums_ref[2]), take(tile_ref[...]))
    out_ref[:, 0:8, :] = top.reshape(owners, 8, 128)
    out_ref[:, 8:16, :] = bottom.reshape(owners, 8, 128)


def put_faces(read, faces, index):
    lane = lax.broadcasted_iota(jnp.int32, (EY, EX), 1)
    low = jnp.zeros((EY, EX), jnp.float32)
    high = jnp.zeros((EY, EX), jnp.float32)
    for x in range(EX):
        plane = read(x)
        low = jnp.where(lane == x, plane[:, 0:1], low)
        high = jnp.where(lane == x, plane[:, EZ - 1 : EZ], high)
        if x == 0:
            faces[1][index] = plane
        if x == EX - 1:
            faces[0][index] = plane
        faces[3][index, x : x + 1, :] = plane[0:1]
        faces[2][index, x : x + 1, :] = plane[EY - 1 : EY]
    faces[5][index] = low
    faces[4][index] = high


def grid_kernel(tile_ref, inc_ref, vel_ref, visc_ref, rhs_ref, *rest):
    faces, (acc_ref,) = rest[:6], rest[6:]
    acc_ref[...] = jnp.zeros_like(acc_ref)

    def add(owner, carry):
        for slot in range(4):
            tile = tile_ref[owner * 4 + slot]
            for c in range(3):
                acc_ref[c, pl.ds(tile, 1), :] += inc_ref[owner, 4 * c + slot : 4 * c + slot + 1, :]
        return carry

    lax.fori_loop(0, inc_ref.shape[0], add, 0)

    def spread(tx, carry):
        rows = pl.ds(pl.multiple_of(tx * 128, 128), 128)
        visc = jnp.exp(acc_ref[1, rows, :] / (1.0 + acc_ref[0, rows, :]))
        for values, out in ((visc, visc_ref), (acc_ref[2, rows, :], rhs_ref)):
            values = swap_blocks(values)
            for ty in range(8):
                for cx in range(4):
                    start = ty * 16 + cx * 4
                    out[tx * 4 + cx, ty * 4 : ty * 4 + 4, :] = values[start : start + 4]
        return carry

    lax.fori_loop(0, 8, spread, 0)
    put_faces(lambda x: visc_ref[x], faces, 0)
    put_faces(lambda x: vel_ref[x], faces, 1)


def sweep_kernel(first, last, coef_ref, field_ref, rhs_ref, visc_ref, *rest):
    visc_faces, rest = rest[:6], rest[6:]
    if first:
        field_faces, field_index = visc_faces, 1
    else:
        field_faces, rest = rest[:6], rest[6:]
        field_index = 0
        old_ref, rest = rest[0], rest[1:]
    out_ref, rest = rest[0], rest[1:]
    row = lax.broadcasted_iota(jnp.int32, (EY, EZ), 0)
    lane = lax.broadcasted_iota(jnp.int32, (EY, EZ), 1)

    def around(ref, faces, index, x):
        plane = ref[x]
        return (
            ref[x - 1] if x > 0 else faces[0][index],
            ref[x + 1] if x < EX - 1 else faces[1][index],
            jnp.where(row == 0, faces[2][index, x : x + 1, :], pltpu.roll(plane, 1, 0)),
            jnp.where(row == EY - 1, faces[3][index, x : x + 1, :], pltpu.roll(plane, EY - 1, 0)),
            jnp.where(lane == 0, faces[4][index, :, x : x + 1], pltpu.roll(plane, 1, 1)),
            jnp.where(lane == EZ - 1, faces[5][index, :, x : x + 1], pltpu.roll(plane, EZ - 1, 1)),
        )

    for x in range(EX):
        field = field_ref[x]
        visc = visc_ref[x]
        flux = jnp.zeros_like(field)
        diagonal = jnp.zeros_like(field)
        for near_visc, near_field in zip(
            around(visc_ref, visc_faces, 0, x), around(field_ref, field_faces, field_index, x)
        ):
            face = 0.5 * (visc + near_visc)
            diagonal = diagonal + face
            flux = flux + face * (field - near_field)
        update = coef_ref[1] * ((rhs_ref[x] - flux) / diagonal)
        if not first:
            update = coef_ref[0] * old_ref[x] + update
        out_ref[x] = field + update
        if not last:
            rest[0][x] = update
    if not last:
        put_faces(lambda x: out_ref[x], rest[1:7], 0)
        return
    tiles_ref, buffer = rest

    def gather(tx, carry):
        for ty in range(8):
            for cx in range(4):
                start = ty * 16 + cx * 4
                buffer[start : start + 4, :] = out_ref[tx * 4 + cx, ty * 4 : ty * 4 + 4, :]
        tiles_ref[pl.ds(pl.multiple_of(tx * 128, 128), 128), :] = swap_blocks(buffer[...])
        return carry

    lax.fori_loop(0, 8, gather, 0)


def pick_kernel(values_ref, cell_ref, count_ref, out_ref):
    for start in range(0, out_ref.shape[0], 8):
        rows = slice(start, start + 8)
        picked = jnp.take_along_axis(
            values_ref[rows, :], cell_ref[rows, :], axis=1, mode="promise_in_bounds"
        )
        slot = lax.broadcasted_iota(jnp.int32, picked.shape, 1)
        out_ref[rows, :] = jnp.where(slot < count_ref[rows, :], picked, 0.0)


def call(kernel, outs, specs, args, scratch=()):
    return pl.pallas_call(
        kernel,
        out_shape=[jax.ShapeDtypeStruct(s, jnp.float32) for s in outs],
        in_specs=[pl.BlockSpec(memory_space=s) for s in specs],
        out_specs=[pl.BlockSpec(memory_space=VMEM)] * len(outs),
        scratch_shapes=[pltpu.VMEM(s, jnp.float32) for s in scratch],
        compiler_params=pltpu.CompilerParams(vmem_limit_bytes=40 * 1024 * 1024),
    )(*args)


def halo_kernel(*refs):
    sources, landings, (send_sem, recv_sem) = refs[:6], refs[6:12], refs[12:]
    barrier = pltpu.get_barrier_semaphore()
    routes = []
    greeted = 0
    for axis, step in SIDES:
        count = lax.axis_size(axis)
        place = lax.axis_index(axis)
        above, below = place < count - 1, place > 0
        sends, receives = (above, below) if step == 1 else (below, above)
        routes.append((sends, receives, {axis: lax.rem(place + step + count, count)}))
        greeted = greeted + jnp.where(sends, 1, 0)
    for sends, _, target in routes:

        @pl.when(sends)
        def _greet():
            pl.semaphore_signal(
                barrier, inc=1, device_id=target, device_id_type=pl.DeviceIdType.MESH
            )

    pl.semaphore_wait(barrier, greeted)

    def copy(k):
        return pltpu.make_async_remote_copy(
            src_ref=sources[k],
            dst_ref=landings[k],
            send_sem=send_sem.at[k],
            recv_sem=recv_sem.at[k],
            device_id=routes[k][2],
            device_id_type=pl.DeviceIdType.MESH,
        )

    for k, (sends, receives, _) in enumerate(routes):

        @pl.when(sends)
        def _start():
            copy(k).start()

        @pl.when(jnp.logical_not(receives))
        def _outside():
            landings[k][...] = jnp.zeros_like(landings[k])

    for k, (sends, receives, _) in enumerate(routes):

        @pl.when(receives)
        def _landed():
            copy(k).wait_recv()

        @pl.when(sends)
        def _left():
            copy(k).wait_send()


def exchange(faces, index):
    return pl.pallas_call(
        halo_kernel,
        out_shape=[jax.ShapeDtypeStruct(f.shape, f.dtype) for f in faces],
        in_specs=[pl.BlockSpec(memory_space=VMEM)] * 6,
        out_specs=[pl.BlockSpec(memory_space=VMEM)] * 6,
        scratch_shapes=[pltpu.SemaphoreType.DMA((6,)), pltpu.SemaphoreType.DMA((6,))],
        compiler_params=pltpu.CompilerParams(collective_id=index, has_side_effects=True),
    )(*faces)


def smooth(velocity, rhs, viscosity, faces, low, high):
    centre = (high + low) / 2
    half_width = (high - low) / 2
    sigma_ratio = centre / half_width
    rho_now = 1.0 / sigma_ratio
    grid = (EX, EY, EZ)
    visc_faces = exchange(faces, 0)
    field, update, field_faces = velocity, None, None
    for index in range(SWEEPS):
        first, last = index == 0, index == SWEEPS - 1
        args = [field, rhs, viscosity, *visc_faces]
        if first:
            coef = jnp.stack([jnp.zeros_like(centre), 1.0 / centre])
        else:
            rho_next = 1.0 / (2.0 * sigma_ratio - rho_now)
            coef = jnp.stack([rho_next * rho_now, 2.0 * rho_next / half_width])
            rho_now = rho_next
            args += [*field_faces, update]
        outs = [grid, (TILES, 128)] if last else [grid, grid] + [(1, *s) for s in FACE_SHAPES]
        results = call(
            functools.partial(sweep_kernel, first, last),
            outs,
            [SMEM] + [VMEM] * len(args),
            [coef, *args],
            [(128, 128)] if last else [],
        )
        if last:
            return results
        field, update = results[:2]
        field_faces = exchange(results[2:], index + 1)


def one_hot_cells(cells):
    return (cells[..., None] == jnp.arange(TILE_CELLS, dtype=jnp.int32)).astype(jnp.float32)


def body(
    velocity,
    marker_logvisc,
    marker_force,
    marker_weight,
    marker_cell,
    block_count,
    block_owner,
    block_tile,
    eig_low,
    eig_high,
):
    blocks, slots = marker_weight.shape
    owners = lax.axis_size("gy") * lax.axis_size("gz")
    capacity = 4
    group = math.gcd(blocks, 64)
    groups = blocks // group
    live = jnp.arange(slots, dtype=jnp.int32)[None, :] < block_count[:, None]
    weight = jnp.where(live, marker_weight, 0.0)
    channels = jnp.stack([weight, weight * marker_logvisc, weight * marker_force])
    channels = channels.reshape(3, groups, group, slots).transpose(1, 0, 2, 3)
    cells_grouped = marker_cell.reshape(groups, group, slots)

    def project(pair):
        cells, values = pair
        return jnp.einsum(
            "gsk,cgs->gck", one_hot_cells(cells), values, precision=lax.Precision.HIGHEST
        )

    block_sums = lax.map(project, (cells_grouped, channels)).reshape(blocks, 3, TILE_CELLS)
    block_sums = block_sums.transpose(1, 0, 2)
    owner = block_owner[:, 0]
    member = (owner[:, None] == jnp.arange(owners, dtype=jnp.int32)[None, :]).astype(jnp.int32)
    slot_of = jnp.sum(jnp.cumsum(member, axis=0) * member, axis=1) - 1
    flat = owner * capacity + slot_of
    tile_wide = jnp.broadcast_to(block_tile.astype(jnp.float32)[:, None], (blocks, 128))
    (outgoing,) = call(
        pack_kernel, [(owners, 16, 128)], [VMEM] * 3, [flat[None, :], tile_wide, block_sums]
    )
    incoming = lax.all_to_all(outgoing, ("gy", "gz"), split_axis=0, concat_axis=0, tiled=True)
    tile_in = incoming[:, 12:16, 0].astype(jnp.int32).reshape(owners * capacity)
    results = call(
        grid_kernel,
        [(EX, EY, EZ)] * 2 + [(2, *s) for s in FACE_SHAPES],
        [SMEM, VMEM, VMEM],
        [tile_in, incoming, velocity],
        [(3, TILES, 128)],
    )
    viscosity, rhs = results[:2]
    smoothed, tile_view = smooth(velocity, rhs, viscosity, results[2:], eig_low[0], eig_high[0])
    returning = tile_view[tile_in].reshape(owners, capacity, TILE_CELLS)
    arrived = lax.all_to_all(returning, ("gy", "gz"), split_axis=0, concat_axis=0, tiled=True)
    counts = jnp.broadcast_to(block_count[:, None], (blocks, slots))
    (marker_velocity,) = call(
        pick_kernel,
        [(blocks, slots)],
        [VMEM] * 3,
        [arrived[owner, slot_of], marker_cell, counts],
    )
    return (smoothed, marker_velocity)


def solution(mesh):
    return jax.shard_map(
        body,
        mesh=mesh,
        in_specs=(
            P("gx", "gy", "gz"),
            P(("gx", "gy", "gz"), None),
            P(("gx", "gy", "gz"), None),
            P(("gx", "gy", "gz"), None),
            P(("gx", "gy", "gz"), None),
            P(("gx", "gy", "gz")),
            P(("gx", "gy", "gz"), None),
            P(("gx", "gy", "gz")),
            P(),
            P(),
        ),
        out_specs=(P("gx", "gy", "gz"), P(("gx", "gy", "gz"), None)),
        check_vma=False,
    )
```
